32 devices in a mesh: group: 8 (over y, x, core), tensor: 4 (over z).
Axes of the slice: x: 2, y: 2, z: 4, core: 2. Of those that a mesh axis runs over, the one named last changes fastest.
Arguments:
- tokens: bfloat16 [8192, 2048], P(('group', 'tensor')), may hold values from -6 to 6
- cotangent: bfloat16 [8192, 2048], P(('group', 'tensor')), may hold values from -6 to 6
- seg_ids: int32 [8192], P('group'), may hold values from 0 to 7, as said below
- live_mask: int32 [8192], P('group'), may hold values from 0 to 1, as said below
- token_counts: int32 [8], replicated, may hold values from 128 to 1024, as said below
- norm1_gain: float32 [2048], replicated, may hold values from 0.1 to 1.9
- norm1_shift: float32 [2048], replicated, may hold values from -3 to 3
- qkv_weight: bfloat16 [3, 2048, 2048], P(None, None, 'tensor'), may hold values from -0.125 to 0.125
- qv_bias: float32 [2, 2048], P(None, 'tensor'), may hold values from -4 to 4
- out_weight: bfloat16 [2048, 2048], P('tensor'), may hold values from -1 to 1
- out_bias: float32 [2048], replicated, may hold values from -4 to 4
- norm2_gain: float32 [2048], replicated, may hold values from 0.1 to 1.9
- norm2_shift: float32 [2048], replicated, may hold values from -3 to 3
- hidden_weight: bfloat16 [2048, 8192], P(None, 'tensor'), may hold values from -0.125 to 0.125
- hidden_bias: float32 [8192], P('tensor'), may hold values from -4 to 4
- down_weight: bfloat16 [8192, 2048], P('tensor'), may hold values from -0.0625 to 0.0625
- down_bias: float32 [2048], replicated, may hold values from -4 to 4
Outputs:
- output: bfloat16 [8192, 2048], P(('group', 'tensor'))
- d_tokens: bfloat16 [8192, 2048], P(('group', 'tensor'))
- grad_norm1_gain: float32 [2048], replicated
- grad_norm1_shift: float32 [2048], replicated
- grad_qkv_weight: float32 [3, 2048, 2048], P(None, None, 'tensor')
- grad_qv_bias: float32 [2, 2048], P(None, 'tensor')
- grad_out_weight: float32 [2048, 2048], P('tensor')
- grad_out_bias: float32 [2048], replicated
- grad_norm2_gain: float32 [2048], replicated
- grad_norm2_shift: float32 [2048], replicated
- grad_hidden_weight: float32 [2048, 8192], P(None, 'tensor')
- grad_hidden_bias: float32 [8192], P('tensor')
- grad_down_weight: float32 [8192, 2048], P('tensor')
- grad_down_bias: float32 [2048], replicated
The draws below stay inside these ranges and needn't reach their ends.
Inputs may be any that keep to these rules, and one draw needn't show every extreme that they name: `seg_ids`: within each group's row the ids start at 0 and rise by 0 or 1 from one token to the next; tokens of equal id in a row form one document; a row holds between 2 and 8 documents of uneven length. In group g's row of 1024 tokens, live_mask is 1 on the first token_counts[g] tokens and 0 on the rest. token_counts[g] is the number of ones of live_mask in group g's row; in every draw one group is full and another holds one eighth of 1024.
All inputs are finite; a program needn't handle non-finite values.
Results may differ from the reference program's by a relative error of at most 0.012.
The reference program's roundings to bfloat16 on the way count: a program that leaves them out, or rounds other values in their place, can miss the bound.
Values may be sent and summed in bfloat16 or wider, within the bound.
No kernel may reach another device: no remote copies, remote signals or barrier semaphores. Data moves between devices by JAX's collectives and lax.ppermute only.
A program may use at most 256 MiB of HBM per device.

```python
import jax
import jax.numpy as jnp
from jax import lax

D = 2048
H = 16
HEAD = 128
FF = 8192
LEN = 1024
GROUPS = 8
TOKENS = 8192


def group_lengths(key):
    base = jax.random.fold_in(key, 17)
    raw_counts = jax.random.randint(jax.random.fold_in(base, 1), (GROUPS,), LEN // 8, LEN + 1)
    order = jax.random.permutation(jax.random.fold_in(base, 2), GROUPS)
    raw_counts = jnp.where(order == 0, LEN, raw_counts)
    raw_counts = jnp.where(order == 1, LEN // 8, raw_counts)
    return raw_counts.astype(jnp.int32)


def draw_token_counts(key, part):
    return group_lengths(key)


def draw_live_mask(key, part):
    lengths = group_lengths(key)
    positions = jnp.arange(LEN, dtype=jnp.int32)
    return (positions[None, :] < lengths[:, None]).astype(jnp.int32).reshape(TOKENS)


def draw_seg_ids(key, part):
    base = jax.random.fold_in(key, 29)
    positions = jnp.arange(LEN, dtype=jnp.int32)
    order = jax.random.permutation(jax.random.fold_in(base, 1), GROUPS)
    doc_counts = jax.random.randint(jax.random.fold_in(base, 2), (GROUPS,), 2, 9).astype(jnp.int32)
    doc_counts = jnp.where(order == 0, 8, doc_counts)
    doc_counts = jnp.where(order == 1, 2, doc_counts).astype(jnp.int32)
    long_len = (LEN // 2 + jax.random.randint(jax.random.fold_in(base, 3), (GROUPS,), 0, LEN // 4)).astype(jnp.int32)
    rest = LEN - long_len
    noise = jax.random.randint(jax.random.fold_in(base, 4), (GROUPS, LEN), 0, 65536).astype(jnp.int32)
    scores = noise * LEN + positions[None, :]
    usable = (positions[None, :] >= 1) & (positions[None, :] < rest[:, None])
    scores = jnp.where(usable, scores, -1)
    picked_scores, cuts = jax.lax.top_k(scores, 6)
    cuts = cuts.astype(jnp.int32)
    slot_ids = jnp.arange(6, dtype=jnp.int32)
    valid = slot_ids[None, :] < (doc_counts - 2)[:, None]
    below = jnp.sum((valid[:, None, :] & (cuts[:, None, :] < cuts[:, :, None])).astype(jnp.int32), axis=2)
    cut_rank = below + 1
    place = jax.random.randint(jax.random.fold_in(base, 5), (GROUPS,), 0, doc_counts).astype(jnp.int32)
    long_start = jnp.sum(jnp.where(valid & (cut_rank == place[:, None]), cuts, 0), axis=1)
    long_start = (long_start + jnp.where(place == doc_counts - 1, rest, 0)).astype(jnp.int32)
    mapped = jnp.where(cuts >= long_start[:, None], cuts + long_len[:, None], cuts)
    mapped = jnp.where(valid, mapped, -1)
    first_short = jnp.where(long_start > 0, -1, long_len)
    long_mark = jnp.where(long_start > 0, long_start, -1)
    marks = jnp.concatenate([mapped, first_short[:, None], long_mark[:, None]], axis=1).astype(jnp.int32)
    starts = jnp.any(positions[None, :, None] == marks[:, None, :], axis=2).astype(jnp.int32)
    return jnp.cumsum(starts, axis=1).astype(jnp.int32).reshape(TOKENS)


def block_levels(rng, extent, shards, low, high):
    def one(axis_at, shards_of):
        heights = jax.random.uniform(jax.random.fold_in(jax.random.fold_in(rng, 6), axis_at), (shards_of,), jnp.float32, low / len(shards), high / len(shards))
        return jnp.repeat(jnp.exp(heights), extent[axis_at] // shards_of).reshape((-1,) + (1,) * (len(extent) - axis_at - 1))

    loudness = one(*shards[0])
    for cut in shards[1:]:
        loudness = loudness * one(*cut)
    return loudness


def scatter_about(key, extent, spread, bound, split=(), kind=jnp.bfloat16):
    array = jax.random.normal(key, extent, jnp.float32) * spread
    if len(split) > 0:
        array = block_levels(key, extent, split, -0.22, 0.18) * array
    return jnp.clip(array, min=-bound, max=bound).astype(kind)


def setup_inputs(seed: int = 0) -> dict:
    streams_of = jax.random.split(jax.random.key(seed), 18)
    tokens = scatter_about(streams_of[0], (TOKENS, D), 1.0, 6.0, ((0, 32),))
    cotangent = scatter_about(streams_of[1], (TOKENS, D), 1.0, 6.0, ((0, 32),))
    seg_ids = draw_seg_ids(jax.random.fold_in(streams_of[17], 71), 0)
    live_mask = draw_live_mask(jax.random.fold_in(streams_of[17], 71), 0)
    token_counts = draw_token_counts(jax.random.fold_in(streams_of[17], 71), 0)
    norm1_gain = jnp.clip(1.0 + 0.18 * jax.random.normal(streams_of[5], (D,), jnp.float32), 0.1, 1.9)
    norm1_shift = scatter_about(streams_of[6], (D,), 0.3, 3.0, (), jnp.float32)
    qkv_weight = scatter_about(streams_of[7], (3, D, H * HEAD), D ** -0.5, 0.125, ((2, 4),))
    qv_bias = scatter_about(streams_of[8], (2, H * HEAD), 0.5, 4.0, ((1, 4),), jnp.float32)
    out_weight = scatter_about(streams_of[9], (H * HEAD, D), (H * HEAD // 64) ** -0.5, 1.0, ((0, 4),))
    out_bias = scatter_about(streams_of[10], (D,), 0.5, 4.0, (), jnp.float32)
    norm2_gain = jnp.clip(1.0 + 0.18 * jax.random.normal(streams_of[11], (D,), jnp.float32), 0.1, 1.9)
    norm2_shift = scatter_about(streams_of[12], (D,), 0.3, 3.0, (), jnp.float32)
    hidden_weight = scatter_about(streams_of[13], (D, FF), D ** -0.5, 0.125, ((1, 4),))
    hidden_bias = scatter_about(streams_of[14], (FF,), 0.5, 4.0, ((0, 4),), jnp.float32)
    down_weight = scatter_about(streams_of[15], (FF, D), FF ** -0.5, 0.0625, ((0, 4),))
    down_bias = scatter_about(streams_of[16], (D,), 0.5, 4.0, (), jnp.float32)
    return dict(tokens=tokens, cotangent=cotangent, seg_ids=seg_ids, live_mask=live_mask, token_counts=token_counts, norm1_gain=norm1_gain, norm1_shift=norm1_shift, qkv_weight=qkv_weight, qv_bias=qv_bias, out_weight=out_weight, out_bias=out_bias, norm2_gain=norm2_gain, norm2_shift=norm2_shift, hidden_weight=hidden_weight, hidden_bias=hidden_bias, down_weight=down_weight, down_bias=down_bias)


@jax.custom_vjp
def low(v):
    return lax.optimization_barrier(v.astype(jnp.bfloat16)).astype(jnp.float32)

@jax.custom_vjp
def low_back(v):
    return v

def low_keep(v):
    return (low(v), None)

def low_pass(kept, grad):
    return (grad,)

def back_keep(v):
    return (v, None)

def back_low(kept, grad):
    return (low(grad),)
low.defvjp(low_keep, low_pass)
low_back.defvjp(back_keep, back_low)
EPSILON = 1e-05
HIGHEST = lax.Precision.HIGHEST

def matmul(left, right):
    return jnp.dot(left, right, precision=HIGHEST)

def layer_norm(values, gain_vec, shift_vec):
    average = lax.optimization_barrier(jnp.mean(values, axis=-1, keepdims=True))
    centred = values - average
    factor = lax.rsqrt(lax.optimization_barrier(jnp.mean(centred * centred, axis=-1, keepdims=True)) + EPSILON)
    return centred * factor * gain_vec + shift_vec

def attention(queries, keys_all, values_all, seg_row, live_row):
    seq_len = queries.shape[0]
    block_rows = min(512, seq_len)
    block_count = seq_len // block_rows
    q_blocks = queries.reshape(block_count, block_rows, H, HEAD)
    key_heads = keys_all.reshape(seq_len, H, HEAD)
    value_heads = values_all.reshape(seq_len, H, HEAD)
    key_pos = jnp.arange(seq_len, dtype=jnp.int32)
    score_scale = HEAD ** (-0.5)

    def one_block(block_item):
        block_index, block_queries = block_item
        first_row = (block_index * block_rows).astype(jnp.int32)
        row_pos = first_row + jnp.arange(block_rows, dtype=jnp.int32)
        seg_rows = lax.dynamic_slice_in_dim(seg_row, first_row, block_rows)
        linked = (seg_rows[:, None] == seg_row[None, :]) & (key_pos[None, :] <= row_pos[:, None]) & (live_row[None, :] > 0)
        allowed = linked | (key_pos[None, :] == row_pos[:, None])
        raw_scores = low_back(jnp.einsum('qhd,khd->hqk', block_queries, key_heads, precision=HIGHEST) * score_scale)
        masked = jnp.where(allowed[None], raw_scores, -1e+30)
        row_max = lax.optimization_barrier(jnp.max(masked, axis=-1, keepdims=True))
        expo_terms = jnp.exp(masked - row_max)
        probs = expo_terms / lax.optimization_barrier(jnp.sum(expo_terms, axis=-1, keepdims=True))
        mixed_block = jnp.einsum('hqk,khd->qhd', low(probs), value_heads, precision=HIGHEST)
        return mixed_block.reshape(block_rows, H * HEAD)
    mixed = lax.map(jax.checkpoint(one_block), (jnp.arange(block_count, dtype=jnp.int32), q_blocks))
    return mixed.reshape(seq_len, H * HEAD)

def row_forward(inputs, norm1_gain, norm1_shift, qkv_weight, qv_bias, out_weight, out_bias, norm2_gain, norm2_shift, hidden_weight, hidden_bias, down_weight, down_bias, seg_row, live_row):
    normed1 = low(layer_norm(inputs, norm1_gain, norm1_shift))
    queries = low(low_back(matmul(normed1, qkv_weight[0]) + qv_bias[0]))
    keys_all = low(low_back(matmul(normed1, qkv_weight[1])))
    values_all = low(low_back(matmul(normed1, qkv_weight[2]) + qv_bias[1]))
    mixed = low(low_back(attention(queries, keys_all, values_all, seg_row, live_row)))
    middle = inputs + low_back(matmul(mixed, out_weight)) + out_bias
    normed2 = low(layer_norm(middle, norm2_gain, norm2_shift))
    hidden_pre = low_back(matmul(normed2, hidden_weight) + hidden_bias)
    activated = low(jax.nn.gelu(hidden_pre, approximate=True))
    return middle + matmul(activated, down_weight) + down_bias

def reference(tokens, cotangent, seg_ids, live_mask, token_counts, norm1_gain, norm1_shift, qkv_weight, qv_bias, out_weight, out_bias, norm2_gain, norm2_shift, hidden_weight, hidden_bias, down_weight, down_bias):
    params = tuple((p.astype(jnp.float32) for p in (norm1_gain, norm1_shift, qkv_weight, qv_bias, out_weight, out_bias, norm2_gain, norm2_shift, hidden_weight, hidden_bias, down_weight, down_bias)))
    count_f = token_counts.astype(jnp.float32)
    share = count_f / jnp.sum(count_f)
    row_inputs = tokens.reshape(GROUPS, LEN, D)
    row_cots = cotangent.reshape(GROUPS, LEN, D)
    row_segs = seg_ids.reshape(GROUPS, LEN)
    row_lives = live_mask.reshape(GROUPS, LEN)

    def one_row(totals, row_item):
        inputs, cot_row, seg_row, live_row, weight = row_item

        def forward(values, *weights):
            return row_forward(values, *weights, seg_row, live_row)
        result, pull = jax.vjp(forward, inputs.astype(jnp.float32), *params)
        grads = pull(cot_row.astype(jnp.float32) * live_row.astype(jnp.float32)[:, None])
        totals = tuple((t + weight * g for t, g in zip(totals, grads[1:])))
        return (totals, (result.astype(jnp.bfloat16), grads[0].astype(jnp.bfloat16)))
    start = tuple((jnp.zeros(p.shape, jnp.float32) for p in params))
    totals, (outputs, d_rows) = lax.scan(one_row, start, (row_inputs, row_cots, row_segs, row_lives, share))
    return (outputs.reshape(TOKENS, D), d_rows.reshape(TOKENS, D), totals[0], totals[1], totals[2], totals[3], totals[4], totals[5], totals[6], totals[7], totals[8], totals[9], totals[10], totals[11])
```

```python
import functools

import jax
import jax.numpy as jnp
from jax import lax
from jax.experimental import pallas as pl
from jax.experimental.pallas import tpu as pltpu
from jax.sharding import PartitionSpec as P

HEAD = 128
EPSILON = 1e-05
MASKED = -1e30
BLOCK = 256
F32 = jnp.float32
BF16 = jnp.bfloat16


def gelu_parts(values):
    root = 0.7978845608028654
    squared = values * values
    tanh = jnp.tanh(root * (values + 0.044715 * (values * squared)))
    half = 0.5 * (1.0 + tanh)
    slope = half + 0.5 * values * (1.0 - tanh * tanh) * (root * (1.0 + 3 * 0.044715 * squared))
    return values * half, slope


def layer_norm(values, gain_vec, shift_vec):
    average = jnp.mean(values, axis=-1, keepdims=True)
    centred = values - average
    factor = lax.rsqrt(jnp.mean(centred * centred, axis=-1, keepdims=True) + EPSILON)
    unit_rows = centred * factor
    return unit_rows * gain_vec + shift_vec, unit_rows, factor


def norm_back(gradient, unit_rows, factor, gain_vec):
    scaled = gradient * gain_vec
    inner_term = (
        scaled
        - jnp.mean(scaled, axis=-1, keepdims=True)
        - unit_rows * jnp.mean(scaled * unit_rows, axis=-1, keepdims=True)
    )
    return factor * inner_term, jnp.sum(gradient * unit_rows, axis=0), jnp.sum(gradient, axis=0)


def dot_nt(left, right):
    return lax.dot_general(left, right, (((1,), (1,)), ((), ())), preferred_element_type=F32)


def masked_scores(keys, block_queries, codes, seg_row, first):
    width, rows = keys.shape[0], block_queries.shape[0]
    raw = dot_nt(keys, block_queries) * (HEAD**-0.5)
    code = jnp.concatenate([codes] * (rows // codes.shape[1]), axis=1)
    key_pos = lax.broadcasted_iota(jnp.int32, (width, rows), 0)
    row_pos = lax.broadcasted_iota(jnp.int32, (width, rows), 1) + first
    allowed = ((code == seg_row) & (key_pos <= row_pos)) | (key_pos == row_pos)
    return jnp.where(allowed, raw, MASKED)


def forward_kernel(qkv_ref, code_ref, seg_ref, mixed_ref, lse_ref):
    length = qkv_ref.shape[1]
    rows = min(BLOCK, length)
    values_t = qkv_ref[2].T
    for first in range(0, length, rows):
        width = first + rows
        span = pl.ds(first, rows)
        scores = masked_scores(
            qkv_ref[1, :width], qkv_ref[0, span], code_ref[:width], seg_ref[:, span], first
        )
        top = jnp.max(scores, axis=0, keepdims=True)
        expo = jnp.exp(scores - top)
        total = jnp.sum(expo, axis=0, keepdims=True)
        probs_low = (expo * (1.0 / total)).astype(BF16)
        mixed_t = jnp.dot(values_t[:, :width], probs_low, preferred_element_type=F32)
        mixed_ref[span, :] = mixed_t.T.astype(BF16)
        lse_ref[0, :, span] = top + jnp.log(total)


def backward_kernel(qkv_ref, code_ref, seg_ref, lse_ref, grad_ref, out_ref, keys_acc, values_acc):
    length = qkv_ref.shape[1]
    rows = min(BLOCK, length)
    scale = HEAD**-0.5
    keys_t = qkv_ref[1].T
    keys_acc[...] = jnp.zeros_like(keys_acc)
    values_acc[...] = jnp.zeros_like(values_acc)
    for first in range(0, length, rows):
        width = first + rows
        span = pl.ds(first, rows)
        block_queries = qkv_ref[0, span]
        block_grad = grad_ref[span, :]
        scores = masked_scores(
            qkv_ref[1, :width], block_queries, code_ref[:width], seg_ref[:, span], first
        )
        probs = jnp.exp(scores - lse_ref[0, :, span])
        d_probs = dot_nt(qkv_ref[2, :width], block_grad)
        delta = jnp.sum(probs * d_probs, axis=0, keepdims=True)
        d_scores = (probs * (d_probs - delta)).astype(BF16)
        d_block = jnp.dot(keys_t[:, :width], d_scores, preferred_element_type=F32)
        out_ref[0, span, :] = (d_block.T * scale).astype(BF16)
        keys_acc[:width] += jnp.dot(d_scores, block_queries, preferred_element_type=F32)
        values_acc[:width] += jnp.dot(probs.astype(BF16), block_grad, preferred_element_type=F32)
    out_ref[1] = (keys_acc[...] * scale).astype(BF16)
    out_ref[2] = values_acc[...].astype(BF16)


def attention_forward(qkv, codes, seg_row):
    _, length, width = qkv.shape
    heads = width // HEAD
    return pl.pallas_call(
        forward_kernel,
        grid=(heads,),
        in_specs=[
            pl.BlockSpec((3, length, HEAD), lambda h: (0, 0, h)),
            pl.BlockSpec(codes.shape, lambda h: (0, 0)),
            pl.BlockSpec(seg_row.shape, lambda h: (0, 0)),
        ],
        out_specs=[
            pl.BlockSpec((length, HEAD), lambda h: (0, h)),
            pl.BlockSpec((1, 1, length), lambda h: (h, 0, 0)),
        ],
        out_shape=[
            jax.ShapeDtypeStruct((length, width), BF16),
            jax.ShapeDtypeStruct((heads, 1, length), F32),
        ],
        name="attention_forward",
    )(qkv, codes, seg_row)


def attention_backward(qkv, codes, seg_row, lse, d_mixed):
    _, length, width = qkv.shape
    heads = width // HEAD
    return pl.pallas_call(
        backward_kernel,
        grid=(heads,),
        in_specs=[
            pl.BlockSpec((3, length, HEAD), lambda h: (0, 0, h)),
            pl.BlockSpec(codes.shape, lambda h: (0, 0)),
            pl.BlockSpec(seg_row.shape, lambda h: (0, 0)),
            pl.BlockSpec((1, 1, length), lambda h: (h, 0, 0)),
            pl.BlockSpec((length, HEAD), lambda h: (0, h)),
        ],
        out_specs=pl.BlockSpec((3, length, HEAD), lambda h: (0, 0, h)),
        out_shape=jax.ShapeDtypeStruct(qkv.shape, BF16),
        scratch_shapes=[pltpu.VMEM((length, HEAD), F32), pltpu.VMEM((length, HEAD), F32)],
        name="attention_backward",
    )(qkv, codes, seg_row, lse, d_mixed)


def swap(values, axis, bit):
    size = lax.axis_size(axis)
    return lax.ppermute(values, axis, [(i, i ^ (1 << bit)) for i in range(size)])


def bit_of(axis, bit):
    return (lax.axis_index(axis) >> bit) & 1


def half_of(values, which):
    rows = values.shape[-2] // 2
    return lax.dynamic_slice_in_dim(values, which * rows, rows, axis=values.ndim - 2)


def joined(own, other, place):
    first = jnp.where(place == 0, own, other)
    second = jnp.where(place == 0, other, own)
    return jnp.concatenate([first, second], axis=own.ndim - 2)


def group_sum(make_half, axis):
    bits = lax.axis_size(axis).bit_length() - 1
    place = bit_of(axis, 0)
    sent = swap(make_half(1 - place).astype(BF16), axis, 0)
    kept = (make_half(place) + sent.astype(F32)).astype(BF16)
    orders = [list(range(1, bits)), list(range(bits - 1, 0, -1))]
    rows = kept.shape[-2] // 2
    streams = [lax.slice_in_dim(kept, s * rows, (s + 1) * rows, axis=kept.ndim - 2) for s in (0, 1)]
    for step in range(bits - 1):
        for s in (0, 1):
            spot = bit_of(axis, orders[s][step])
            other = swap(half_of(streams[s], 1 - spot), axis, orders[s][step])
            streams[s] = (half_of(streams[s], spot).astype(F32) + other.astype(F32)).astype(BF16)
    for step in range(bits - 2, -1, -1):
        for s in (0, 1):
            other = swap(streams[s], axis, orders[s][step])
            streams[s] = joined(streams[s], other, bit_of(axis, orders[s][step]))
    kept = jnp.concatenate(streams, axis=kept.ndim - 2)
    return joined(kept, swap(kept, axis, 0), place).astype(F32)


def small_sum(values, axis):
    for bit in range(lax.axis_size(axis).bit_length() - 1):
        values = values + swap(values, axis, bit)
    return values


def shards(
    tokens,
    cotangent,
    seg_ids,
    live_mask,
    token_counts,
    norm1_gain,
    norm1_shift,
    qkv_weight,
    qv_bias,
    out_weight,
    out_bias,
    norm2_gain,
    norm2_shift,
    hidden_weight,
    hidden_bias,
    down_weight,
    down_bias,
):
    own_rows, model = tokens.shape
    first_row = lax.axis_index("tensor") * own_rows
    live_own = lax.dynamic_slice_in_dim(live_mask, first_row, own_rows)
    count_f = token_counts.astype(F32)
    chosen = jnp.arange(count_f.shape[0], dtype=jnp.int32) == lax.axis_index("group")
    weight = jnp.sum(jnp.where(chosen, count_f, 0.0)) / jnp.sum(count_f)
    codes = jnp.broadcast_to(
        jnp.where(live_mask > 0, seg_ids, -1)[:, None], (seg_ids.shape[0], 128)
    )
    seg_row = seg_ids[None, :]

    inputs = tokens.astype(F32)
    normed1, unit1, factor1 = layer_norm(inputs, norm1_gain, norm1_shift)
    gathered1 = lax.all_gather(normed1.astype(BF16), "tensor", axis=0, tiled=True)
    bias3 = jnp.stack([qv_bias[0], jnp.zeros_like(qv_bias[0]), qv_bias[1]])
    qkv = (
        jnp.einsum("ld,sdh->slh", gathered1, qkv_weight, preferred_element_type=F32)
        + bias3[:, None, :]
    ).astype(BF16)
    mixed, lse = attention_forward(qkv, codes, seg_row)
    attn_own = lax.psum_scatter(
        jnp.dot(mixed, out_weight, preferred_element_type=F32).astype(BF16),
        "tensor",
        scatter_dimension=0,
        tiled=True,
    ).astype(F32)
    middle = inputs + attn_own + out_bias
    normed2, unit2, factor2 = layer_norm(middle, norm2_gain, norm2_shift)
    gathered2 = lax.all_gather(normed2.astype(BF16), "tensor", axis=0, tiled=True)
    masked_cot = cotangent * live_own[:, None].astype(BF16)
    cot_own = masked_cot.astype(F32)
    d_output = lax.all_gather(masked_cot, "tensor", axis=0, tiled=True)

    hidden_pre = jnp.dot(gathered2, hidden_weight, preferred_element_type=F32) + hidden_bias
    gelu_value, gelu_slope = gelu_parts(hidden_pre)
    activated = gelu_value.astype(BF16)
    d_activated = jnp.einsum("ld,fd->lf", d_output, down_weight, preferred_element_type=F32)
    d_hidden = (d_activated * gelu_slope).astype(BF16)
    d_normed2 = lax.psum_scatter(
        jnp.einsum("lf,df->ld", d_hidden, hidden_weight, preferred_element_type=F32).astype(BF16),
        "tensor",
        scatter_dimension=0,
        tiled=True,
    ).astype(F32)
    mlp_own = lax.psum_scatter(
        jnp.dot(activated, down_weight, preferred_element_type=F32).astype(BF16),
        "tensor",
        scatter_dimension=0,
        tiled=True,
    ).astype(F32)
    output = (middle + mlp_own + down_bias).astype(BF16)

    def weight_grad(spec, left, right):
        def make_half(which):
            cols = left.shape[1] // 2
            part = lax.dynamic_slice_in_dim(left, which * cols, cols, axis=1)
            return weight * jnp.einsum(spec, part, right, preferred_element_type=F32)

        return group_sum(make_half, "group")

    sum_down = weight_grad("lf,ld->fd", activated, d_output)
    sum_hidden = weight_grad("ld,lf->df", gathered2, d_hidden)

    via_norm2, grad_gain2, grad_shift2 = norm_back(d_normed2, unit2, factor2, norm2_gain)
    d_middle = cot_own + via_norm2
    d_attn = lax.all_gather(d_middle.astype(BF16), "tensor", axis=0, tiled=True)
    d_mixed = jnp.einsum("ld,hd->lh", d_attn, out_weight, preferred_element_type=F32).astype(BF16)
    d_qkv = attention_backward(qkv, codes, seg_row, lse, d_mixed)
    d_normed1 = lax.psum_scatter(
        jnp.einsum("slh,sdh->ld", d_qkv, qkv_weight, preferred_element_type=F32).astype(BF16),
        "tensor",
        scatter_dimension=0,
        tiled=True,
    ).astype(F32)
    sum_out = weight_grad("lh,ld->hd", mixed, d_attn)
    sum_qkv = weight_grad("ld,slh->sdh", gathered1, d_qkv)

    via_norm1, grad_gain1, grad_shift1 = norm_back(d_normed1, unit1, factor1, norm1_gain)
    d_tokens = (d_middle + via_norm1).astype(BF16)

    grad_qv = jnp.stack(
        [jnp.sum(d_qkv[0].astype(F32), axis=0), jnp.sum(d_qkv[2].astype(F32), axis=0)]
    )
    grad_hidden_bias = jnp.sum(d_hidden.astype(F32), axis=0)
    early = jnp.stack(
        [jnp.sum(d_middle, axis=0), grad_gain2, grad_shift2, jnp.sum(cot_own, axis=0)]
    )
    early = small_sum(weight * early, "tensor")
    biases = weight * grad_hidden_bias
    early = small_sum(jnp.concatenate([early.reshape(-1), biases]).reshape(-1, 128), "group")
    early = early.reshape(-1)
    vectors = early[: 4 * model].reshape(4, model)
    sum_hidden_bias = early[4 * model :]
    late = small_sum(weight * jnp.stack([grad_gain1, grad_shift1]), "tensor")
    late = small_sum(
        jnp.concatenate([late.reshape(-1), weight * grad_qv.reshape(-1)]).reshape(-1, 128), "group"
    ).reshape(-1)
    sum_qv = late[2 * model :].reshape(qv_bias.shape)
    return (
        output,
        d_tokens,
        late[:model],
        late[model : 2 * model],
        sum_qkv,
        sum_qv,
        sum_out,
        vectors[0],
        vectors[1],
        vectors[2],
        sum_hidden,
        sum_hidden_bias,
        sum_down,
        vectors[3],
    )


def solution(mesh):
    both = P(("group", "tensor"), None)
    return jax.shard_map(
        shards,
        mesh=mesh,
        in_specs=(
            both,
            both,
            P("group"),
            P("group"),
            P(),
            P(),
            P(),
            P(None, None, "tensor"),
            P(None, "tensor"),
            P("tensor", None),
            P(),
            P(),
            P(),
            P(None, "tensor"),
            P("tensor"),
            P("tensor", None),
            P(),
        ),
        out_specs=(
            both,
            both,
            P(),
            P(),
            P(None, None, "tensor"),
            P(None, "tensor"),
            P("tensor", None),
            P(),
            P(),
            P(),
            P(None, "tensor"),
            P("tensor"),
            P("tensor", None),
            P(),
        ),
        check_vma=False,
    )
```

```python
import functools

import jax
import jax.numpy as jnp
from jax import lax
from jax.experimental import pallas as pl
from jax.experimental.pallas import tpu as pltpu
from jax.sharding import PartitionSpec as P


HEAD = 128
EPSILON = 1e-05
MASKED = -1e30
BLOCK = 256
F32 = jnp.float32
BF16 = jnp.bfloat16


def gelu_parts(values):
    root = 0.7978845608028654
    squared = values * values
    tanh = jnp.tanh(root * (values + 0.044715 * (values * squared)))
    half = 0.5 * (1.0 + tanh)
    slope = half + 0.5 * values * (1.0 - tanh * tanh) * (root * (1.0 + 3 * 0.044715 * squared))
    return values * half, slope


def layer_norm(values, gain_vec, shift_vec):
    average = jnp.mean(values, axis=-1, keepdims=True)
    centred = values - average
    factor = lax.rsqrt(jnp.mean(centred * centred, axis=-1, keepdims=True) + EPSILON)
    unit_rows = centred * factor
    return unit_rows * gain_vec + shift_vec, unit_rows, factor


def norm_back(gradient, unit_rows, factor, gain_vec):
    scaled = gradient * gain_vec
    inner_term = (
        scaled
        - jnp.mean(scaled, axis=-1, keepdims=True)
        - unit_rows * jnp.mean(scaled * unit_rows, axis=-1, keepdims=True)
    )
    return factor * inner_term, jnp.sum(gradient * unit_rows, axis=0), jnp.sum(gradient, axis=0)


def dot_nt(left, right):
    return lax.dot_general(left, right, (((1,), (1,)), ((), ())), preferred_element_type=F32)


def masked_scores(keys, block_queries, codes, seg_row, first):
    width, rows = keys.shape[0], block_queries.shape[0]
    raw = dot_nt(keys, block_queries) * (HEAD**-0.5)
    code = jnp.concatenate([codes] * (rows // codes.shape[1]), axis=1)
    key_pos = lax.broadcasted_iota(jnp.int32, (width, rows), 0)
    row_pos = lax.broadcasted_iota(jnp.int32, (width, rows), 1) + first
    allowed = ((code == seg_row) & (key_pos <= row_pos)) | (key_pos == row_pos)
    return jnp.where(allowed, raw, MASKED)


def forward_kernel(qkv_ref, code_ref, seg_ref, mixed_ref, lse_ref):
    length = qkv_ref.shape[1]
    rows = min(BLOCK, length)
    values_t = qkv_ref[2].T
    for first in range(0, length, rows):
        width = first + rows
        span = pl.ds(first, rows)
        scores = masked_scores(
            qkv_ref[1, :width], qkv_ref[0, span], code_ref[:width], seg_ref[:, span], first
        )
        top = jnp.max(scores, axis=0, keepdims=True)
        expo = jnp.exp(scores - top)
        total = jnp.sum(expo, axis=0, keepdims=True)
        probs_low = (expo * (1.0 / total)).astype(BF16)
        mixed_t = jnp.dot(values_t[:, :width], probs_low, preferred_element_type=F32)
        mixed_ref[span, :] = mixed_t.T.astype(BF16)
        lse_ref[0, :, span] = top + jnp.log(total)


def backward_kernel(qkv_ref, code_ref, seg_ref, lse_ref, grad_ref, out_ref, keys_acc, values_acc):
    length = qkv_ref.shape[1]
    rows = min(BLOCK, length)
    scale = HEAD**-0.5
    keys_t = qkv_ref[1].T
    keys_acc[...] = jnp.zeros_like(keys_acc)
    values_acc[...] = jnp.zeros_like(values_acc)
    for first in range(0, length, rows):
        width = first + rows
        span = pl.ds(first, rows)
        block_queries = qkv_ref[0, span]
        block_grad = grad_ref[span, :]
        scores = masked_scores(
            qkv_ref[1, :width], block_queries, code_ref[:width], seg_ref[:, span], first
        )
        probs = jnp.exp(scores - lse_ref[0, :, span])
        d_probs = dot_nt(qkv_ref[2, :width], block_grad)
        delta = jnp.sum(probs * d_probs, axis=0, keepdims=True)
        d_scores = (probs * (d_probs - delta)).astype(BF16)
        d_block = jnp.dot(keys_t[:, :width], d_scores, preferred_element_type=F32)
        out_ref[0, span, :] = (d_block.T * scale).astype(BF16)
        keys_acc[:width] += jnp.dot(d_scores, block_queries, preferred_element_type=F32)
        values_acc[:width] += jnp.dot(probs.astype(BF16), block_grad, preferred_element_type=F32)
    out_ref[1] = (keys_acc[...] * scale).astype(BF16)
    out_ref[2] = values_acc[...].astype(BF16)


def attention_forward(qkv, codes, seg_row):
    _, length, width = qkv.shape
    heads = width // HEAD
    return pl.pallas_call(
        forward_kernel,
        grid=(heads,),
        in_specs=[
            pl.BlockSpec((3, length, HEAD), lambda h: (0, 0, h)),
            pl.BlockSpec(codes.shape, lambda h: (0, 0)),
            pl.BlockSpec(seg_row.shape, lambda h: (0, 0)),
        ],
        out_specs=[
            pl.BlockSpec((length, HEAD), lambda h: (0, h)),
            pl.BlockSpec((1, 1, length), lambda h: (h, 0, 0)),
        ],
        out_shape=[
            jax.ShapeDtypeStruct((length, width), BF16),
            jax.ShapeDtypeStruct((heads, 1, length), F32),
        ],
        name="attention_forward",
    )(qkv, codes, seg_row)


def attention_backward(qkv, codes, seg_row, lse, d_mixed):
    _, length, width = qkv.shape
    heads = width // HEAD
    return pl.pallas_call(
        backward_kernel,
        grid=(heads,),
        in_specs=[
            pl.BlockSpec((3, length, HEAD), lambda h: (0, 0, h)),
            pl.BlockSpec(codes.shape, lambda h: (0, 0)),
            pl.BlockSpec(seg_row.shape, lambda h: (0, 0)),
            pl.BlockSpec((1, 1, length), lambda h: (h, 0, 0)),
            pl.BlockSpec((length, HEAD), lambda h: (0, h)),
        ],
        out_specs=pl.BlockSpec((3, length, HEAD), lambda h: (0, 0, h)),
        out_shape=jax.ShapeDtypeStruct(qkv.shape, BF16),
        scratch_shapes=[pltpu.VMEM((length, HEAD), F32), pltpu.VMEM((length, HEAD), F32)],
        name="attention_backward",
    )(qkv, codes, seg_row, lse, d_mixed)


def swap(values, axis, bit):
    size = lax.axis_size(axis)
    return lax.ppermute(values, axis, [(i, i ^ (1 << bit)) for i in range(size)])


def bit_of(axis, bit):
    return (lax.axis_index(axis) >> bit) & 1


def half_of(values, which):
    rows = values.shape[-2] // 2
    return lax.dynamic_slice_in_dim(values, which * rows, rows, axis=values.ndim - 2)


def assemble_kernel(streams, place_ref, *refs):
    own, other, out_ref = refs[:streams], refs[streams : 2 * streams], refs[-1]
    mine = pl.program_id(1) == place_ref[0]
    for s in range(streams):
        chosen = pl.program_id(2) == s

        @pl.when(chosen & mine)
        def _(s=s):
            out_ref[...] = own[s][...].astype(out_ref.dtype)

        @pl.when(chosen & jnp.logical_not(mine))
        def _(s=s):
            out_ref[...] = other[s][...].astype(out_ref.dtype)


def assemble(own, other, place, dtype):
    streams = len(own)
    planes, rows, cols = own[0].shape
    block = min(rows, max(16, (1 << 20) // cols))
    count = rows // block

    def spec(s, wanted):
        def index(p, half, stream, i, place_ref):
            live = (stream == s) & ((half == place_ref[0]) == wanted)
            return p, jnp.where(live, i, 0), 0

        return pl.BlockSpec((1, block, cols), index)

    return pl.pallas_call(
        functools.partial(assemble_kernel, streams),
        grid_spec=pltpu.PrefetchScalarGridSpec(
            num_scalar_prefetch=1,
            grid=(planes, 2, streams, count),
            in_specs=[spec(s, True) for s in range(streams)]
            + [spec(s, False) for s in range(streams)],
            out_specs=pl.BlockSpec(
                (1, block, cols),
                lambda p, half, stream, i, place_ref: (p, (half * streams + stream) * count + i, 0),
            ),
        ),
        out_shape=jax.ShapeDtypeStruct((planes, 2 * streams * rows, cols), dtype),
        name="assemble",
    )(place[None].astype(jnp.int32), *own, *other)


def after(values, *others):
    return lax.optimization_barrier((values, *others))[0] if others else values


def chip_sum(make_half, axis):
    place = bit_of(axis, 0)
    sent = swap(make_half(1 - place).astype(BF16), axis, 0)
    kept = (make_half(place) + sent.astype(F32)).astype(BF16)
    return kept.reshape((-1,) + kept.shape[-2:])


def link_orders(axis):
    bits = lax.axis_size(axis).bit_length() - 1
    return [list(range(1, bits)), list(range(bits - 1, 0, -1))]


def reduce_streams(kept, axis):
    orders = link_orders(axis)
    rows = kept.shape[1] // 2
    streams = [lax.slice_in_dim(kept, s * rows, (s + 1) * rows, axis=1) for s in (0, 1)]
    for bits in zip(*orders):
        for s in (0, 1):
            spot = bit_of(axis, bits[s])
            other = swap(half_of(streams[s], 1 - spot), axis, bits[s])
            streams[s] = (half_of(streams[s], spot).astype(F32) + other.astype(F32)).astype(BF16)
    return streams


def copy_streams(streams, axis, skip=0, stop=None):
    orders = link_orders(axis)
    streams = list(streams)
    for bits in list(zip(*(order[::-1] for order in orders)))[skip:stop]:
        for s in (0, 1):
            other = swap(streams[s], axis, bits[s])
            streams[s] = assemble([streams[s]], [other], bit_of(axis, bits[s]), BF16)
    return streams


def join_cores(streams, axis):
    others = [swap(part, axis, 0) for part in streams]
    return assemble(streams, others, bit_of(axis, 0), F32)


def line_steps(axis):
    size = lax.axis_size(axis)
    right = lambda first, last: [(i, i + 1) for i in range(first, last)]
    left = lambda first, last: [(i + 1, i) for i in range(first, last)]
    return size, right, left


def collect_kernel(size, here_ref, *refs):
    own_ref, left_refs, right_refs, out_ref = refs[0], refs[1:size], refs[size:-1], refs[-1]
    ahead = pl.program_id(0) - here_ref[0]

    @pl.when(ahead == 0)
    def _():
        out_ref[...] = own_ref[...]

    for step in range(1, size):

        @pl.when(ahead == -step)
        def _(step=step):
            out_ref[...] = left_refs[step - 1][...]

        @pl.when(ahead == step)
        def _(step=step):
            out_ref[...] = right_refs[step - 1][...]


def line_copies(own, axis):
    size, right, left = line_steps(axis)
    from_left, from_right = [own], [own]
    for step in range(1, size):
        from_left.append(lax.ppermute(from_left[-1], axis, right(step - 1, size - 1)))
        from_right.append(lax.ppermute(from_right[-1], axis, left(0, size - step)))
    return from_left[1:], from_right[1:]


def line_collect(own, from_left, from_right, axis):
    size = lax.axis_size(axis)
    rows, cols = own.shape
    blocks = [own] + from_left + from_right
    return pl.pallas_call(
        functools.partial(collect_kernel, size),
        grid_spec=pltpu.PrefetchScalarGridSpec(
            num_scalar_prefetch=1,
            grid=(size,),
            in_specs=[pl.BlockSpec((rows, cols), lambda i, here_ref: (0, 0)) for _ in blocks],
            out_specs=pl.BlockSpec((rows, cols), lambda i, here_ref: (i, 0)),
        ),
        out_shape=jax.ShapeDtypeStruct((size * rows, cols), own.dtype),
        name="collect",
    )(lax.axis_index(axis)[None].astype(jnp.int32), *blocks)


def small_sum(values, axis):
    for bit in range(lax.axis_size(axis).bit_length() - 1):
        values = values + swap(values, axis, bit)
    return values


def layer(
    tokens,
    cotangent,
    seg_ids,
    live_mask,
    token_counts,
    norm1_gain,
    norm1_shift,
    qkv_weight,
    qv_bias,
    out_weight,
    out_bias,
    norm2_gain,
    norm2_shift,
    hidden_weight,
    hidden_bias,
    down_weight,
    down_bias,
):
    own_rows, model = tokens.shape
    first_row = lax.axis_index("tensor") * own_rows
    live_own = lax.dynamic_slice_in_dim(live_mask, first_row, own_rows)
    count_f = token_counts.astype(F32)
    chosen = jnp.arange(count_f.shape[0], dtype=jnp.int32) == lax.axis_index("group")
    weight = jnp.sum(jnp.where(chosen, count_f, 0.0)) / jnp.sum(count_f)
    codes = jnp.broadcast_to(
        jnp.where(live_mask > 0, seg_ids, -1)[:, None], (seg_ids.shape[0], 128)
    )
    seg_row = seg_ids[None, :]

    inputs = tokens.astype(F32)
    normed1, unit1, factor1 = layer_norm(inputs, norm1_gain, norm1_shift)
    gathered1 = lax.all_gather(normed1.astype(BF16), "tensor", axis=0, tiled=True)
    bias3 = jnp.stack([qv_bias[0], jnp.zeros_like(qv_bias[0]), qv_bias[1]])
    qkv = (
        jnp.einsum("ld,sdh->slh", gathered1, qkv_weight, preferred_element_type=F32)
        + bias3[:, None, :]
    ).astype(BF16)
    mixed, lse = attention_forward(qkv, codes, seg_row)

    masked_cot = cotangent * live_own[:, None].astype(BF16)
    cot_own = masked_cot.astype(F32)

    def scatter(partial):
        return lax.psum_scatter(partial, "tensor", scatter_dimension=0, tiled=True).astype(F32)

    def gather(block):
        return lax.all_gather(block, "tensor", axis=0, tiled=True)

    cot_left, cot_right = line_copies(after(masked_cot, gathered1), "tensor")
    attn_own = scatter(
        jnp.dot(
            after(mixed, cot_left[0], cot_right[0]), out_weight, preferred_element_type=F32
        ).astype(BF16)
    )
    attn_own = after(attn_own, cot_left[1], cot_right[1])
    middle = inputs + attn_own + out_bias
    normed2, unit2, factor2 = layer_norm(middle, norm2_gain, norm2_shift)
    gathered2 = gather(normed2.astype(BF16))
    d_output = line_collect(masked_cot, cot_left, cot_right, "tensor")
    gathered2 = after(gathered2, d_output)

    hidden_pre = jnp.dot(gathered2, hidden_weight, preferred_element_type=F32) + hidden_bias
    gelu_value, gelu_slope = gelu_parts(hidden_pre)
    activated = gelu_value.astype(BF16)
    d_activated = jnp.einsum("ld,fd->lf", d_output, down_weight, preferred_element_type=F32)
    d_hidden = (d_activated * gelu_slope).astype(BF16)
    d_normed2 = scatter(
        jnp.einsum("lf,df->ld", d_hidden, hidden_weight, preferred_element_type=F32).astype(BF16)
    )

    def half_grad(spec, left, right):
        def make_half(which):
            cols = left.shape[1] // 2
            part = lax.dynamic_slice_in_dim(left, which * cols, cols, axis=1)
            return weight * jnp.einsum(spec, part, right, preferred_element_type=F32)

        return chip_sum(make_half, "group")

    kept_down = half_grad("lf,ld->fd", activated, d_output)
    kept_hidden = half_grad("ld,lf->df", gathered2, d_hidden)
    mlp = jnp.dot(activated, down_weight, preferred_element_type=F32).astype(BF16)

    d_normed2 = after(d_normed2, kept_down, kept_hidden, mlp)
    via_norm2, grad_gain2, grad_shift2 = norm_back(d_normed2, unit2, factor2, norm2_gain)
    d_middle = cot_own + via_norm2
    d_low = d_middle.astype(BF16)
    d_attn = gather(d_low)

    down_streams = reduce_streams(kept_down, "group")
    hidden_streams = reduce_streams(kept_hidden, "group")
    d_attn = after(d_attn, *down_streams, *hidden_streams)

    d_mixed = jnp.einsum("ld,hd->lh", d_attn, out_weight, preferred_element_type=F32).astype(BF16)
    d_qkv = attention_backward(qkv, codes, seg_row, lse, d_mixed)
    down_streams = copy_streams(down_streams, "group", 0, 1)
    hidden_streams = copy_streams(hidden_streams, "group", 0, 1)
    d_qkv = after(d_qkv, *down_streams, *hidden_streams)
    partial1 = jnp.einsum("slh,sdh->ld", d_qkv, qkv_weight, preferred_element_type=F32)
    partial1 = partial1.astype(BF16)

    mlp_own = scatter(after(mlp, d_attn))
    output = (middle + mlp_own + down_bias).astype(BF16)
    d_normed1 = scatter(after(partial1, mlp_own))

    down_streams = copy_streams(down_streams, "group", 1)
    hidden_streams = copy_streams(hidden_streams, "group", 1)
    kept_qkv = half_grad(
        "ld,slh->sdh", gathered1, after(d_qkv, partial1, *down_streams, *hidden_streams)
    )
    kept_out = half_grad("lh,ld->hd", mixed, after(d_attn, kept_qkv))
    sum_down = join_cores(down_streams, "group")[0]
    sum_hidden = join_cores(hidden_streams, "group")[0]
    out_streams = copy_streams(reduce_streams(kept_out, "group"), "group")
    qkv_streams = reduce_streams(kept_qkv, "group")
    qkv_streams = [after(part, sum_down) for part in qkv_streams]
    qkv_streams = copy_streams(qkv_streams, "group")
    qkv_streams = [after(part, sum_hidden) for part in qkv_streams]
    sum_out = join_cores(out_streams, "group")[0]
    sum_qkv = join_cores(qkv_streams, "group")
    all_d_hidden = d_hidden

    via_norm1, grad_gain1, grad_shift1 = norm_back(d_normed1, unit1, factor1, norm1_gain)
    d_tokens = (d_middle + via_norm1).astype(BF16)

    grad_qv = jnp.stack(
        [jnp.sum(d_qkv[0].astype(F32), axis=0), jnp.sum(d_qkv[2].astype(F32), axis=0)]
    )
    grad_hidden_bias = jnp.sum(all_d_hidden.astype(F32), axis=0)
    early = jnp.stack(
        [jnp.sum(d_middle, axis=0), grad_gain2, grad_shift2, jnp.sum(cot_own, axis=0)]
    )
    early = small_sum(weight * early, "tensor")
    biases = weight * grad_hidden_bias
    early = small_sum(jnp.concatenate([early.reshape(-1), biases]).reshape(-1, 128), "group")
    early = early.reshape(-1)
    vectors = early[: 4 * model].reshape(4, model)
    sum_hidden_bias = early[4 * model :]
    late = small_sum(weight * jnp.stack([grad_gain1, grad_shift1]), "tensor")
    late = small_sum(
        jnp.concatenate([late.reshape(-1), weight * grad_qv.reshape(-1)]).reshape(-1, 128), "group"
    ).reshape(-1)
    sum_qv = late[2 * model :].reshape(qv_bias.shape)
    return (
        output,
        d_tokens,
        late[:model],
        late[model : 2 * model],
        sum_qkv,
        sum_qv,
        sum_out,
        vectors[0],
        vectors[1],
        vectors[2],
        sum_hidden,
        sum_hidden_bias,
        sum_down,
        vectors[3],
    )


def solution(mesh):
    both = P(("group", "tensor"), None)
    return jax.shard_map(
        layer,
        mesh=mesh,
        in_specs=(
            both,
            both,
            P("group"),
            P("group"),
            P(),
            P(),
            P(),
            P(None, None, "tensor"),
            P(None, "tensor"),
            P("tensor", None),
            P(),
            P(),
            P(),
            P(None, "tensor"),
            P("tensor"),
            P("tensor", None),
            P(),
        ),
        out_specs=(
            both,
            both,
            P(),
            P(),
            P(None, None, "tensor"),
            P(None, "tensor"),
            P("tensor", None),
            P(),
            P(),
            P(),
            P(None, "tensor"),
            P("tensor"),
            P("tensor", None),
            P(),
        ),
        check_vma=False,
    )
```
